32 devices in a mesh: visit: 2 (over core), tx: 4 (over y, x), ty: 4 (over z).
Axes of the slice: x: 2, y: 2, z: 4, core: 2. Of those that a mesh axis runs over, the one named last changes fastest.
Arguments:
- raw: bfloat16 [4, 2048, 2048], P('visit', ('tx', 'ty')), may hold values from -12 to 12, as said below
- dark: float32 [2048, 2048], P(('tx', 'ty')), may hold values from 0 to 0.8
- flat: float32 [2048, 2048], P(('tx', 'ty')), may hold values from 0.5 to 1.5
- mask: int32 [4, 2048, 2048], P('visit', ('tx', 'ty')), may hold values 0 or 1
- offsets: int32 [4, 2], P('visit'), may hold values from 0 to 255
- scales: float32 [4, 2], P('visit'), may hold values from 0.985 to 1.015
- fracs: float32 [4, 2], P('visit'), may hold values from 0 to 1
Outputs:
- coadd: float32 [2048, 2048], P('visit', ('tx', 'ty'))
The draws below stay inside these ranges and needn't reach their ends.
Inputs may be any that keep to these rules, and one draw needn't show every extreme that they name: `raw`: each exposure's pixels have a noise level of its own.
All inputs are finite; a program needn't handle non-finite values. No bound on the sum of `mask` on one device may be relied on, other than what follows from the above.
Results may differ from the reference program's by a relative error of at most 0.00145.
The reference program's roundings to bfloat16 on the way count: a program that leaves them out, or rounds other values in their place, can miss the bound.
Values may be sent and summed in bfloat16 or wider, within the bound.
A program may use at most 64 MiB of HBM per device.

```python
import jax
import jax.numpy as jnp

P_SIZE = 2048
NEXP = 4
OFFSET = 256


def draw_raw(key, part):
    key_level = jax.random.fold_in(key, 11)
    key_noise = jax.random.fold_in(key, 12)
    levels = jnp.exp(jax.random.uniform(key_level, (NEXP, 1, 1), jnp.float32, jnp.log(0.5), jnp.log(2.0)))
    values = jnp.clip(jax.random.normal(key_noise, (NEXP, P_SIZE, P_SIZE), jnp.float32), -6.0, 6.0)
    return (values * levels).astype(jnp.bfloat16)


def place_ends(drawn, rng, smallest, top_value):
    longest = drawn.shape.index(max(drawn.shape))
    spots = []
    for shift in (0, 1):
        where = [jax.random.randint(jax.random.fold_in(rng, axis), (), 0, length) for axis, length in enumerate(drawn.shape)]
        where[longest] = (where[longest] + shift) % drawn.shape[longest]
        spots.append(tuple(where))
    return drawn.at[spots[0]].set(smallest).at[spots[1]].set(top_value)


def level_of(own_key, extent, split, smallest, top_value):
    loudness = 1.0
    for axis_at, blocks in split:
        steps = jax.random.uniform(jax.random.fold_in(jax.random.fold_in(own_key, 6), axis_at), (blocks,), jnp.float32, smallest / len(split), top_value / len(split))
        loudness = loudness * jnp.repeat(jnp.exp(steps), extent[axis_at] // blocks).reshape((-1,) + (1,) * (len(extent) - 1 - axis_at))
    return loudness


def setup_inputs(seed: int = 0) -> dict:
    keys = jax.random.split(jax.random.key(seed), 8)
    raw = draw_raw(jax.random.fold_in(keys[7], 71), 0)
    dark = jnp.clip(0.8 * jax.random.uniform(keys[1], (P_SIZE, P_SIZE), jnp.float32) ** level_of(keys[1], (P_SIZE, P_SIZE), ((0, 16),), -0.2, 0.2), 0.0, 0.8)
    flat = jnp.clip(1.0 + 0.1 * jax.random.normal(keys[2], (P_SIZE, P_SIZE), jnp.float32), 0.5, 1.5)
    mask = place_ends((jax.random.randint(keys[3], (NEXP, P_SIZE, P_SIZE), 0, 16) < 15).astype(jnp.int32), jax.random.fold_in(keys[3], 1), 0, 1)
    offsets = place_ends(jax.random.randint(keys[4], (NEXP, 2), 0, OFFSET), jax.random.fold_in(keys[4], 1), 0, OFFSET - 1).astype(jnp.int32)
    scales = jnp.clip(0.985 + 0.029999971 * jax.random.uniform(keys[5], (NEXP, 2), jnp.float32) ** level_of(keys[5], (NEXP, 2), ((0, 2),), -0.2, 0.2), 0.985, 1.015)
    fracs = jnp.clip(1.0 * jax.random.uniform(keys[6], (NEXP, 2), jnp.float32) ** level_of(keys[6], (NEXP, 2), ((0, 2),), -0.2, 0.2), 0.0, 1.0)
    return {"raw": raw, "dark": dark, "flat": flat, "mask": mask, "offsets": offsets, "scales": scales, "fracs": fracs}


def lanczos(offsets_t):
    return jnp.where(jnp.abs(offsets_t) < 3.0, jnp.sinc(offsets_t) * jnp.sinc(offsets_t / 3.0), 0.0)


def warp_last(image, offset, scale, frac):
    sky = jnp.arange(P_SIZE, dtype=jnp.float32)
    coords = (sky - offset.astype(jnp.float32)) * scale + frac
    base = jnp.floor(coords).astype(jnp.int32)
    total = jnp.zeros(image.shape, jnp.float32)
    for step in range(-2, 4):
        index = base + step
        taps = lanczos(coords - index.astype(jnp.float32)).astype(jnp.bfloat16).astype(jnp.float32)
        valid = (index >= 0) & (index < P_SIZE)
        clipped = jnp.clip(index, 0, P_SIZE - 1).astype(jnp.int32)
        total = total + image[:, clipped] * jnp.where(valid, taps, 0.0)[None, :]
    return total


def reference(raw, dark, flat, mask, offsets, scales, fracs):
    numerator = jnp.zeros((P_SIZE, P_SIZE), jnp.float32)
    denominator = jnp.zeros((P_SIZE, P_SIZE), jnp.float32)
    for expo in range(NEXP):
        good = mask[expo].astype(jnp.float32)
        corrected = (raw[expo].astype(jnp.float32) - dark) * flat * good
        sumsq = jnp.sum(corrected * corrected)
        count = jnp.sum(good)
        weight = count / (sumsq + 1e-5 * count)
        image16 = corrected.astype(jnp.bfloat16).astype(jnp.float32)
        colwarped = warp_last(image16, offsets[expo, 1], scales[expo, 1], fracs[expo, 1]).astype(jnp.bfloat16)
        colcover = warp_last(good, offsets[expo, 1], scales[expo, 1], fracs[expo, 1]).astype(jnp.bfloat16)
        warped = warp_last(colwarped.astype(jnp.float32).T, offsets[expo, 0], scales[expo, 0], fracs[expo, 0]).T
        cover = warp_last(colcover.astype(jnp.float32).T, offsets[expo, 0], scales[expo, 0], fracs[expo, 0]).T
        numerator = numerator + weight * warped
        denominator = denominator + weight * cover
    return numerator / jnp.maximum(denominator, 1.0)
```

```python
import functools
import math

import jax
import jax.numpy as jnp
from jax import lax
from jax.experimental import pallas as pl
from jax.experimental.pallas import tpu as pltpu
from jax.sharding import PartitionSpec as P

MESH = pl.DeviceIdType.MESH
BLOCK = 128
COL_ALIGN = 128
ROW_ALIGN = 32
SINE = [(-1) ** n * math.pi ** (2 * n + 1) / math.factorial(2 * n + 1) for n in range(6)]


def window_size(frame_len, align):
    return min(frame_len, -(-(3 * frame_len // 100 + BLOCK + 267 + align) // 128) * 128)


def sin_pi(t):
    near = jnp.floor(t + 0.5)
    r = t - near
    r2 = r * r
    total = jnp.full_like(r, SINE[-1])
    for c in SINE[-2::-1]:
        total = total * r2 + c
    odd = near - 2.0 * jnp.floor(near * 0.5)
    return total * r * (1.0 - 2.0 * odd)


def lanczos(t):
    safe = jnp.where(jnp.abs(t) < 1e-4, 1.0, t)
    value = sin_pi(safe) * sin_pi(safe / 3.0) * (3.0 / math.pi**2) / (safe * safe)
    value = jnp.where(jnp.abs(t) < 1e-4, 1.0, value)
    return jnp.where(jnp.abs(t) < 3.0, value, 0.0)


def banded(taps, first, window):
    frame = (lax.broadcasted_iota(jnp.int32, (window, taps.shape[1]), 0) + first).astype(jnp.float32)
    step = frame - taps[6:7, :]
    total = jnp.zeros_like(step)
    for tap in range(6):
        total = jnp.where(step == float(tap - 2), taps[tap : tap + 1, :], total)
    return total.astype(jnp.bfloat16)


def window_start(sky, frame_len, window, align):
    lowest = lax.div(lax.max((sky - 255) * 197 - 800, 0), 200)
    return pl.multiple_of(lax.min(lax.div(lowest, align) * align, frame_len - window), align)


def kernel(dims, offsets, scales, fracs, raw_in, dark_in, flat_in, mask_in, out, *scratch):
    exposures, parts, band, frame_len, visits, n_tx, n_ty, relay = dims
    raw, dark, flat, mask, taps, rowk, image, outgoing, stats, totals, partial = scratch[:11]
    rest = list(scratch[11:])
    strips = [rest.pop(0) for _ in range(exposures)]
    in_sem, send_sem, recv_sem, stat_send, stat_recv, sum_send, sum_recv = [rest.pop(0) for _ in range(7)]
    if relay:
        auxs = [rest.pop(0) for _ in range(exposures)]
        fills = [rest.pop(0) for _ in range(exposures)]
        aux_totals, aux_partial, relay_out, relay_in = [rest.pop(0) for _ in range(4)]
        aux_recv, aux_send, aux_sum_recv, relay_send, relay_recv = [rest.pop(0) for _ in range(5)]
    width = frame_len // parts
    col_window, row_window = window_size(frame_len, COL_ALIGN), window_size(frame_len, ROW_ALIGN)
    vi, ti, yi = lax.axis_index("visit"), lax.axis_index("tx"), lax.axis_index("ty")
    me = ti * n_ty + yi
    own = frame_len // visits
    blocks = own // BLOCK

    if relay:
        high = lax.div(yi, 2)
        depth = high * (3 - yi) + (1 - high) * yi
        inner = depth == 1
        outer = depth == 0
        hub_y, far_y = 1 + high, 3 * (1 - high)
        far_strip = ti * n_ty + far_y

    loads = [(dark_in, dark), (flat_in, flat)]
    for expo in range(exposures):
        loads += [(raw_in.at[expo], raw.at[expo]), (mask_in.at[expo], mask.at[expo])]
    loads = [pltpu.make_async_copy(src, dst, in_sem.at[n]) for n, (src, dst) in enumerate(loads)]
    barrier = pltpu.get_barrier_semaphore()

    def peer(step):
        at = lax.rem(me + step, parts)
        return (vi, lax.div(at, n_ty), lax.rem(at, n_ty))

    def greet(step, carry):
        pl.semaphore_signal(barrier, inc=1, device_id=peer(step), device_id_type=MESH)
        return carry

    def greet_visit(step, carry):
        to = (lax.rem(vi + step, visits), ti, yi)
        pl.semaphore_signal(barrier, inc=1, device_id=to, device_id_type=MESH)
        return carry

    lax.fori_loop(1, parts, greet, 0)
    lax.fori_loop(1, visits, greet_visit, 0)
    for load in loads:
        load.start()

    def weigh(expo, axis):
        shape = (8, frame_len)
        sky = lax.broadcasted_iota(jnp.int32, shape, 1).astype(jnp.float32)
        tap = lax.broadcasted_iota(jnp.int32, shape, 0).astype(jnp.float32)
        offset = offsets[expo, axis].astype(jnp.float32)
        coords = (sky - offset) * scales[expo, axis] + fracs[expo, axis]
        base = jnp.floor(coords)
        values = lanczos(coords - (base + (tap - 2.0)))
        taps[expo, axis, :, :] = jnp.where(tap < 6.0, values, base)

    def correct(expo):
        def chunk(at, carry):
            sumsq, count = carry
            cols = pl.ds(pl.multiple_of(at * 128, 128), 128)
            good = mask[expo, :, cols].astype(jnp.float32)
            fixed = (raw[expo, :, cols].astype(jnp.float32) - dark[:, cols]) * flat[:, cols] * good
            image[expo, 0:band, cols] = fixed.astype(jnp.bfloat16)
            image[expo, band : 2 * band, cols] = good.astype(jnp.bfloat16)
            sumsq = sumsq + jnp.sum(fixed * fixed, axis=0, keepdims=True)
            count = count + jnp.sum(good, axis=0, keepdims=True)
            return sumsq, count

        zero = jnp.zeros((1, 128), jnp.float32)
        sumsq, count = lax.fori_loop(0, frame_len // 128, chunk, (zero, zero))
        stats[me, expo : expo + 1, :] = sumsq
        stats[me, exposures + expo : exposures + expo + 1, :] = count

    def band_rows(source):
        return pl.ds(pl.multiple_of(source * band, band), band)

    def strip_copy(expo, strip, source, to, via=False):
        return pltpu.make_async_remote_copy(
            src_ref=outgoing.at[expo, strip],
            dst_ref=(auxs if via else strips)[expo].at[band_rows(source), :],
            send_sem=send_sem.at[expo, strip],
            recv_sem=(aux_recv if via else recv_sem).at[expo, source],
            device_id=to,
            device_id_type=MESH,
        )

    def stat_copy(source, step):
        return pltpu.make_async_remote_copy(
            src_ref=stats.at[source],
            dst_ref=stats.at[source],
            send_sem=stat_send.at[step],
            recv_sem=stat_recv.at[source],
            device_id=peer(step),
            device_id_type=MESH,
        )

    def column_kernel(expo, strip):
        first = window_start(strip * width, frame_len, col_window, COL_ALIGN)
        cols = pl.ds(pl.multiple_of(strip * width, width), width)
        return first, banded(taps[expo, 1, :, cols], first, col_window)

    def column(expo, strip):
        first, k = column_kernel(expo, strip)
        operand = image[expo, :, pl.ds(first, col_window)]
        return jnp.dot(operand, k, preferred_element_type=jnp.float32).astype(jnp.bfloat16)

    def put(ref, both):
        ref[:, 0:width] = both[0:band]
        ref[:, width : 2 * width] = both[band : 2 * band]

    if relay:
        groups = [(0, 0, 1), (1, 0, 1), (0, 1, 3), (1, 1, 3)]

        def target(index, head):
            group, over = lax.div(index, n_tx), lax.rem(index, n_tx)
            if head:
                reach = group * 0 + 3
            else:
                reach = lax.select(inner, lax.rem(2 * group + 2, 4) - lax.div(group, 2), 2 - group)
            via = reach == 3
            to_t = lax.rem(ti + over, n_tx)
            strip_y = high * (3 - reach) + (1 - high) * reach
            to_y = lax.select(via, hub_y, strip_y)
            return to_t * n_ty + strip_y, (vi, to_t, to_y), via, (to_t == ti) & (to_y == yi)

        def prepare(expo, index, head):
            strip, to, via, mine = target(index, head)
            both = column(expo, strip)

            @pl.when(jnp.logical_not(mine))
            def _():
                put(outgoing.at[expo, strip], both)

            @pl.when(mine & via)
            def _():
                put(auxs[expo].at[band_rows(me), :], both)

            @pl.when(mine & jnp.logical_not(via))
            def _():
                put(strips[expo].at[band_rows(me), :], both)

        def dispatch(expo, index, head, start):
            strip, to, via, mine = target(index, head)

            @pl.when(jnp.logical_not(mine) & via)
            def _():
                copy = strip_copy(expo, strip, me, to, True)
                copy.start() if start else copy.wait_send()

            @pl.when(jnp.logical_not(mine) & jnp.logical_not(via))
            def _():
                copy = strip_copy(expo, strip, me, to, False)
                copy.start() if start else copy.wait_send()

    else:
        groups = [(expo, 1, n_ty) for expo in range(exposures)]

        def target(index, head):
            group, over = lax.div(index, n_tx), lax.rem(index, n_tx)
            to_t, to_y = lax.rem(ti + over, n_tx), lax.rem(yi + group, n_ty)
            return to_t * n_ty + to_y, (vi, to_t, to_y), (to_t == ti) & (to_y == yi)

        def prepare(expo, index, head):
            strip, to, mine = target(index, head)
            both = column(expo, strip)

            @pl.when(jnp.logical_not(mine))
            def _():
                put(outgoing.at[expo, strip], both)

            @pl.when(mine)
            def _():
                put(strips[expo].at[band_rows(me), :], both)

        def dispatch(expo, index, head, start):
            strip, to, mine = target(index, head)

            @pl.when(jnp.logical_not(mine))
            def _():
                copy = strip_copy(expo, strip, me, to)
                copy.start() if start else copy.wait_send()

    def over_group(group, *actions):
        expo, tail, length = group

        def step(index, carry):
            for action in actions:
                action(expo, index, tail == 0)
            return carry

        lax.fori_loop(0, length * n_tx, step, 0)

    def begin(expo, index, head):
        dispatch(expo, index, head, True)

    def finish_send(expo, index, head):
        dispatch(expo, index, head, False)

    for expo in range(exposures):
        weigh(expo, 1)
    loads[0].wait()
    loads[1].wait()
    for expo in range(exposures):
        loads[2 + 2 * expo].wait()
        loads[3 + 2 * expo].wait()
        correct(expo)
    if relay:
        over_group(groups[0], prepare)
    pl.semaphore_wait(barrier, parts + visits - 2)

    def send_stat(step, carry):
        stat_copy(me, step).start()
        return carry

    lax.fori_loop(1, parts, send_stat, 0)
    if relay:
        over_group(groups[0], begin)
    for group in groups[1 if relay else 0 :]:
        over_group(group, prepare, begin)

    for expo in range(exposures):
        weigh(expo, 0)

        def build(block, carry, expo=expo):
            at = pl.multiple_of(block * BLOCK, BLOCK)
            first = window_start(at, frame_len, row_window, ROW_ALIGN)
            rowk[expo, pl.ds(at, BLOCK), :] = banded(taps[expo, 0, :, pl.ds(at, BLOCK)], first, row_window).T
            return carry

        lax.fori_loop(0, frame_len // BLOCK, build, 0)

    def wait_stat(step, carry):
        stat_copy(lax.rem(me + step, parts), step).wait()
        return carry

    lax.fori_loop(1, parts, wait_stat, 0)
    sums = jnp.sum(jnp.sum(stats[...], axis=0), axis=1, keepdims=True)
    weights, full = [], []
    for expo in range(exposures):
        count = sums[exposures + expo : exposures + expo + 1, :]
        weights.append(count / (sums[expo : expo + 1, :] + 1e-05 * count))
        full.append(jnp.where(2.0 * count >= float(frame_len * frame_len), 1.0, 0.0))

    def warp(expo, at, source):
        first = window_start(at, frame_len, row_window, ROW_ALIGN)
        return jnp.dot(
            rowk[expo, pl.ds(at, BLOCK), :],
            source[pl.ds(first, row_window), :],
            preferred_element_type=jnp.float32,
        )

    def block_rows(block):
        return pl.ds(pl.multiple_of(block * BLOCK, BLOCK), BLOCK)

    if relay:
        half_rows = 2 * band
        fill_strip = lax.select(inner, far_strip, me)

        def half_at(index, side):
            return pl.ds(pl.multiple_of(index * n_ty * band + side * half_rows, half_rows), half_rows)

        for expo in range(exposures):
            _, k = column_kernel(expo, fill_strip)
            cover = jnp.sum(k.astype(jnp.float32), axis=0, keepdims=True).astype(jnp.bfloat16)
            cover = cover.astype(jnp.float32) * full[expo]
            cover = jnp.broadcast_to(cover, (half_rows, width)).astype(jnp.bfloat16)
            blank = jnp.zeros((half_rows, width), jnp.bfloat16)

            @pl.when(inner)
            def _(expo=expo, cover=cover, blank=blank):
                for index in range(n_tx):
                    auxs[expo][half_at(index, 1 - high), 0:width] = blank
                    auxs[expo][half_at(index, 1 - high), width : 2 * width] = blank
                    fills[expo][half_at(index, 1 - high), :] = blank
                    fills[expo][half_at(index, high), :] = cover

            @pl.when(outer)
            def _(expo=expo, cover=cover, blank=blank):
                for index in range(n_tx):
                    strips[expo][half_at(index, 1 - high), 0:width] = blank
                    strips[expo][half_at(index, 1 - high), width : 2 * width] = cover

        def half_band(index):
            return lax.div(index, 2) * n_ty + high * 2 + lax.rem(index, 2)

        def aux_sum_copy(block):
            at = pl.multiple_of((1 - vi) * own + block * BLOCK, BLOCK)
            return pltpu.make_async_remote_copy(
                src_ref=aux_totals.at[pl.ds(at, BLOCK), :],
                dst_ref=aux_partial.at[block_rows(block), :],
                send_sem=aux_send.at[block],
                recv_sem=aux_sum_recv.at[block],
                device_id=(1 - vi, ti, yi),
                device_id_type=MESH,
            )

        def relay_copy(block):
            return pltpu.make_async_remote_copy(
                src_ref=relay_out.at[block_rows(block), :],
                dst_ref=relay_in.at[block_rows(block), :],
                send_sem=relay_send.at[block],
                recv_sem=relay_recv.at[block],
                device_id=(vi, ti, far_y),
                device_id_type=MESH,
            )

        def aux_row(at):
            at = pl.multiple_of(at, BLOCK)
            value = cover = 0.0
            for expo in range(exposures):
                both = warp(expo, at, auxs[expo])
                value = value + weights[expo] * both[:, 0:width]
                cover = cover + weights[expo] * (both[:, width : 2 * width] - warp(expo, at, fills[expo]))
            aux_totals[pl.ds(at, BLOCK), 0:width] = value
            aux_totals[pl.ds(at, BLOCK), width : 2 * width] = cover

        @pl.when(inner)
        def _():
            for expo in range(exposures):

                def wait_aux(index, carry, expo=expo):
                    source = half_band(index)

                    @pl.when(source != me)
                    def _():
                        strip_copy(expo, 0, source, (vi, ti, yi), True).wait_recv()

                    return carry

                lax.fori_loop(0, parts // 2, wait_aux, 0)

            def other_half(block, carry):
                aux_row((1 - vi) * own + block * BLOCK)
                aux_sum_copy(block).start()
                return carry

            def own_half(block, carry):
                at = pl.multiple_of(vi * own + block * BLOCK, BLOCK)
                aux_row(at)
                aux_sum_copy(block).wait()
                total = aux_totals[pl.ds(at, BLOCK), :] + aux_partial[block_rows(block), :]
                relay_out[block_rows(block), :] = total.astype(jnp.bfloat16)
                relay_copy(block).start()
                return carry

            lax.fori_loop(0, blocks, other_half, 0)
            lax.fori_loop(0, blocks, own_half, 0)

    def sum_copy(step, block):
        to = lax.rem(vi + step, visits)
        at = pl.multiple_of(to * own + block * BLOCK, BLOCK)
        return pltpu.make_async_remote_copy(
            src_ref=totals.at[pl.ds(at, BLOCK), :],
            dst_ref=partial.at[step, block_rows(block), :],
            send_sem=sum_send.at[step, block],
            recv_sem=sum_recv.at[step, block],
            device_id=(to, ti, yi),
            device_id_type=MESH,
        )

    for expo in range(exposures):

        def wait_strip(step, carry, expo=expo):
            source = lax.rem(me + step, parts)
            if relay:

                @pl.when(inner | (lax.div(lax.rem(source, n_ty), 2) == high))
                def _():
                    strip_copy(expo, 0, source, (vi, ti, yi)).wait_recv()

            else:
                strip_copy(expo, 0, source, (vi, ti, yi)).wait_recv()
            return carry

        lax.fori_loop(1, parts, wait_strip, 0)
        last = expo == exposures - 1

        def row(at, expo=expo):
            at = pl.multiple_of(at, BLOCK)
            warped = weights[expo] * warp(expo, at, strips[expo])
            rows = pl.ds(at, BLOCK)
            totals[rows, :] = warped if expo == 0 else totals[rows, :] + warped

        def row_step(index, carry, row=row, last=last):
            step, block = lax.div(index, blocks) + 1, lax.rem(index, blocks)
            row(lax.rem(vi + step, visits) * own + block * BLOCK)
            if last:
                sum_copy(step, block).start()
            return carry

        def own_row(block, carry, row=row):
            row(vi * own + block * BLOCK)
            return carry

        lax.fori_loop(0, (visits - 1) * blocks, row_step, 0)
        lax.fori_loop(0, blocks, own_row, 0)

    def finish(block, carry):
        total = totals[pl.ds(pl.multiple_of(vi * own + block * BLOCK, BLOCK), BLOCK), :]
        for step in range(1, visits):
            sum_copy(step, block).wait()
            total = total + partial[step, block_rows(block), :]
        if relay:
            totals[pl.ds(pl.multiple_of(vi * own + block * BLOCK, BLOCK), BLOCK), :] = total

            @pl.when(outer)
            def _():
                relay_copy(block).wait_recv()
                at = pl.ds(pl.multiple_of(vi * own + block * BLOCK, BLOCK), BLOCK)
                totals[at, :] = total + relay_in[block_rows(block), :].astype(jnp.float32)

            total = totals[pl.ds(pl.multiple_of(vi * own + block * BLOCK, BLOCK), BLOCK), :]
        out[block_rows(block), :] = total[:, 0:width] / jnp.maximum(total[:, width : 2 * width], 1.0)
        return carry

    lax.fori_loop(0, blocks, finish, 0)

    for group in groups:
        over_group(group, finish_send)
    if relay:

        @pl.when(inner)
        def _():
            def sent(block, carry):
                relay_copy(block).wait_send()
                return carry

            lax.fori_loop(0, blocks, sent, 0)


def shards(n_visit, n_tx, n_ty, raw, dark, flat, mask, offsets, scales, fracs):
    exposures, band, frame_len = raw.shape
    parts = n_tx * n_ty
    width = frame_len // parts
    own = frame_len // n_visit
    blocks = own // BLOCK
    relay = n_visit == 2 and n_ty == 4 and exposures == 2
    row_window = window_size(frame_len, ROW_ALIGN)
    smem = pl.BlockSpec(memory_space=pltpu.SMEM)
    vmem = pl.BlockSpec(memory_space=pltpu.VMEM)
    dims = (exposures, parts, band, frame_len, n_visit, n_tx, n_ty, relay)
    dma = pltpu.SemaphoreType.DMA
    scratch = [
        pltpu.VMEM(raw.shape, raw.dtype),
        pltpu.VMEM(dark.shape, dark.dtype),
        pltpu.VMEM(flat.shape, flat.dtype),
        pltpu.VMEM(mask.shape, mask.dtype),
        pltpu.VMEM((exposures, 2, 8, frame_len), jnp.float32),
        pltpu.VMEM((exposures, frame_len, row_window), jnp.bfloat16),
        pltpu.VMEM((exposures, 2 * band, frame_len), jnp.bfloat16),
        pltpu.VMEM((exposures, parts, band, 2 * width), jnp.bfloat16),
        pltpu.VMEM((parts, 2 * exposures, 128), jnp.float32),
        pltpu.VMEM((frame_len, 2 * width), jnp.float32),
        pltpu.VMEM((n_visit, own, 2 * width), jnp.float32),
    ]
    scratch += [pltpu.VMEM((frame_len, 2 * width), jnp.bfloat16)] * exposures
    scratch += [
        dma((2 + 2 * exposures,)),
        dma((exposures, parts)),
        dma((exposures, parts)),
        dma((parts,)),
        dma((parts,)),
        dma((n_visit, blocks)),
        dma((n_visit, blocks)),
    ]
    if relay:
        scratch += [pltpu.VMEM((frame_len, 2 * width), jnp.bfloat16)] * exposures
        scratch += [pltpu.VMEM((frame_len, width), jnp.bfloat16)] * exposures
        scratch += [
            pltpu.VMEM((frame_len, 2 * width), jnp.float32),
            pltpu.VMEM((own, 2 * width), jnp.float32),
            pltpu.VMEM((own, 2 * width), jnp.bfloat16),
            pltpu.VMEM((own, 2 * width), jnp.bfloat16),
            dma((exposures, parts)),
            dma((blocks,)),
            dma((blocks,)),
            dma((blocks,)),
            dma((blocks,)),
        ]
    return pl.pallas_call(
        functools.partial(kernel, dims),
        out_shape=jax.ShapeDtypeStruct((own, width), jnp.float32),
        in_specs=[smem] * 3 + [pl.BlockSpec(memory_space=pl.ANY)] * 4,
        out_specs=vmem,
        scratch_shapes=scratch,
        compiler_params=pltpu.CompilerParams(
            collective_id=0, has_side_effects=True, vmem_limit_bytes=60000000
        ),
    )(offsets, scales, fracs, raw, dark, flat, mask)


def solution(mesh):
    in_specs = (
        P("visit", ("tx", "ty"), None),
        P(("tx", "ty"), None),
        P(("tx", "ty"), None),
        P("visit", ("tx", "ty"), None),
        P("visit", None),
        P("visit", None),
        P("visit", None),
    )
    out_specs = P("visit", ("tx", "ty"))
    body = functools.partial(shards, mesh.shape["visit"], mesh.shape["tx"], mesh.shape["ty"])
    return jax.shard_map(body, mesh=mesh, in_specs=in_specs, out_specs=out_specs, check_vma=False)
```

```python
import functools
import math

import jax
import jax.numpy as jnp
from jax import lax
from jax.experimental import pallas as pl
from jax.experimental.pallas import tpu as pltpu
from jax.sharding import PartitionSpec as P

MESH = pl.DeviceIdType.MESH
BLOCK = 128
COL_ALIGN = 128
ROW_ALIGN = 32
SINE = [(-1) ** n * math.pi ** (2 * n + 1) / math.factorial(2 * n + 1) for n in range(6)]


def window_size(frame_len, align):
    return min(frame_len, -(-(3 * frame_len // 100 + BLOCK + 267 + align) // 128) * 128)


def sin_pi(t):
    near = jnp.floor(t + 0.5)
    r = t - near
    r2 = r * r
    total = jnp.full_like(r, SINE[-1])
    for c in SINE[-2::-1]:
        total = total * r2 + c
    odd = near - 2.0 * jnp.floor(near * 0.5)
    return total * r * (1.0 - 2.0 * odd)


def lanczos(t):
    safe = jnp.where(jnp.abs(t) < 1e-4, 1.0, t)
    value = sin_pi(safe) * sin_pi(safe / 3.0) * (3.0 / math.pi**2) / (safe * safe)
    value = jnp.where(jnp.abs(t) < 1e-4, 1.0, value)
    return jnp.where(jnp.abs(t) < 3.0, value, 0.0)


def banded(taps, first, window):
    frame = (lax.broadcasted_iota(jnp.int32, (window, taps.shape[1]), 0) + first).astype(jnp.float32)
    step = frame - taps[6:7, :]
    total = jnp.zeros_like(step)
    for tap in range(6):
        total = jnp.where(step == float(tap - 2), taps[tap : tap + 1, :], total)
    return total.astype(jnp.bfloat16)


def window_start(sky, frame_len, window, align):
    lowest = lax.div(lax.max((sky - 255) * 197 - 800, 0), 200)
    return pl.multiple_of(lax.min(lax.div(lowest, align) * align, frame_len - window), align)


def kernel(dims, offsets, scales, fracs, raw_in, dark_in, flat_in, mask_in, out, *scratch):
    exposures, parts, band, frame_len, visits, n_tx, n_ty, relay = dims
    raw, dark, flat, mask, taps, rowk, image, outgoing, stats, totals, partial = scratch[:11]
    rest = list(scratch[11:])
    strips = [rest.pop(0) for _ in range(exposures)]
    in_sem, send_sem, recv_sem, stat_send, stat_recv, sum_send, sum_recv = [rest.pop(0) for _ in range(7)]
    if relay:
        auxs = [rest.pop(0) for _ in range(exposures)]
        fills = [rest.pop(0) for _ in range(exposures)]
        aux_totals, aux_partial, relay_out, relay_in = [rest.pop(0) for _ in range(4)]
        aux_recv, aux_send, aux_sum_recv, relay_send, relay_recv = [rest.pop(0) for _ in range(5)]
    width = frame_len // parts
    col_window, row_window = window_size(frame_len, COL_ALIGN), window_size(frame_len, ROW_ALIGN)
    vi, ti, yi = lax.axis_index("visit"), lax.axis_index("tx"), lax.axis_index("ty")
    me = ti * n_ty + yi
    own = frame_len // visits
    blocks = own // BLOCK

    if relay:
        high = lax.div(yi, 2)
        depth = high * (3 - yi) + (1 - high) * yi
        inner = depth == 1
        outer = depth == 0
        hub_y, far_y = 1 + high, 3 * (1 - high)
        far_strip = ti * n_ty + far_y

    loads = [(dark_in, dark), (flat_in, flat)]
    for expo in range(exposures):
        loads += [(raw_in.at[expo], raw.at[expo]), (mask_in.at[expo], mask.at[expo])]
    loads = [pltpu.make_async_copy(src, dst, in_sem.at[n]) for n, (src, dst) in enumerate(loads)]
    barrier = pltpu.get_barrier_semaphore()

    def peer(step):
        at = lax.rem(me + step, parts)
        return (vi, lax.div(at, n_ty), lax.rem(at, n_ty))

    def greet(step, carry):
        pl.semaphore_signal(barrier, inc=1, device_id=peer(step), device_id_type=MESH)
        return carry

    def greet_visit(step, carry):
        to = (lax.rem(vi + step, visits), ti, yi)
        pl.semaphore_signal(barrier, inc=1, device_id=to, device_id_type=MESH)
        return carry

    lax.fori_loop(1, parts, greet, 0)
    lax.fori_loop(1, visits, greet_visit, 0)
    for load in loads:
        load.start()

    def weigh(expo, axis):
        shape = (8, frame_len)
        sky = lax.broadcasted_iota(jnp.int32, shape, 1).astype(jnp.float32)
        tap = lax.broadcasted_iota(jnp.int32, shape, 0).astype(jnp.float32)
        offset = offsets[expo, axis].astype(jnp.float32)
        coords = (sky - offset) * scales[expo, axis] + fracs[expo, axis]
        base = jnp.floor(coords)
        values = lanczos(coords - (base + (tap - 2.0)))
        taps[expo, axis, :, :] = jnp.where(tap < 6.0, values, base)

    def correct(expo):
        def chunk(at, carry):
            sumsq, count = carry
            cols = pl.ds(pl.multiple_of(at * 128, 128), 128)
            good = mask[expo, :, cols].astype(jnp.float32)
            fixed = (raw[expo, :, cols].astype(jnp.float32) - dark[:, cols]) * flat[:, cols] * good
            image[expo, 0:band, cols] = fixed.astype(jnp.bfloat16)
            image[expo, band : 2 * band, cols] = good.astype(jnp.bfloat16)
            sumsq = sumsq + jnp.sum(fixed * fixed, axis=0, keepdims=True)
            count = count + jnp.sum(good, axis=0, keepdims=True)
            return sumsq, count

        zero = jnp.zeros((1, 128), jnp.float32)
        sumsq, count = lax.fori_loop(0, frame_len // 128, chunk, (zero, zero))
        stats[me, expo : expo + 1, :] = sumsq
        stats[me, exposures + expo : exposures + expo + 1, :] = count

    def band_rows(source):
        return pl.ds(pl.multiple_of(source * band, band), band)

    def strip_copy(expo, strip, source, to, via=False):
        return pltpu.make_async_remote_copy(
            src_ref=outgoing.at[expo, strip],
            dst_ref=(auxs if via else strips)[expo].at[band_rows(source), :],
            send_sem=send_sem.at[expo, strip],
            recv_sem=(aux_recv if via else recv_sem).at[expo, source],
            device_id=to,
            device_id_type=MESH,
        )

    def stat_copy(source, step):
        return pltpu.make_async_remote_copy(
            src_ref=stats.at[source],
            dst_ref=stats.at[source],
            send_sem=stat_send.at[step],
            recv_sem=stat_recv.at[source],
            device_id=peer(step),
            device_id_type=MESH,
        )

    def column_kernel(expo, strip):
        first = window_start(strip * width, frame_len, col_window, COL_ALIGN)
        cols = pl.ds(pl.multiple_of(strip * width, width), width)
        return first, banded(taps[expo, 1, :, cols], first, col_window)

    def column(expo, strip):
        first, k = column_kernel(expo, strip)
        operand = image[expo, :, pl.ds(first, col_window)]
        return jnp.dot(operand, k, preferred_element_type=jnp.float32).astype(jnp.bfloat16)

    def put(ref, both):
        ref[:, 0:width] = both[0:band]
        ref[:, width : 2 * width] = both[band : 2 * band]

    if relay:
        groups = [(0, True, 0, 4), (1, True, 0, 4), (0, False, 0, 4), (1, False, 0, 4), (0, False, 4, 12), (1, False, 4, 12)]

        def target(index, head):
            group, over = lax.div(index, n_tx), lax.rem(index, n_tx)
            if head:
                reach = group * 0 + 3
            else:
                reach = lax.select(inner, lax.rem(2 * group + 2, 4) - lax.div(group, 2), 2 - group)
            via = reach == 3
            to_t = lax.rem(ti + over, n_tx)
            strip_y = high * (3 - reach) + (1 - high) * reach
            to_y = lax.select(via, hub_y, strip_y)
            return to_t * n_ty + strip_y, (vi, to_t, to_y), via, (to_t == ti) & (to_y == yi)

        def prepare(expo, index, head):
            strip, to, via, mine = target(index, head)
            both = column(expo, strip)

            @pl.when(jnp.logical_not(mine))
            def _():
                put(outgoing.at[expo, strip], both)

            @pl.when(mine & via)
            def _():
                put(auxs[expo].at[band_rows(me), :], both)

            @pl.when(mine & jnp.logical_not(via))
            def _():
                put(strips[expo].at[band_rows(me), :], both)

        def dispatch(expo, index, head, start):
            strip, to, via, mine = target(index, head)

            @pl.when(jnp.logical_not(mine) & via)
            def _():
                copy = strip_copy(expo, strip, me, to, True)
                copy.start() if start else copy.wait_send()

            @pl.when(jnp.logical_not(mine) & jnp.logical_not(via))
            def _():
                copy = strip_copy(expo, strip, me, to, False)
                copy.start() if start else copy.wait_send()

    else:
        groups = [(expo, False, 0, n_tx * n_ty) for expo in range(exposures)]

        def target(index, head):
            group, over = lax.div(index, n_tx), lax.rem(index, n_tx)
            to_t, to_y = lax.rem(ti + over, n_tx), lax.rem(yi + group, n_ty)
            return to_t * n_ty + to_y, (vi, to_t, to_y), (to_t == ti) & (to_y == yi)

        def prepare(expo, index, head):
            strip, to, mine = target(index, head)
            both = column(expo, strip)

            @pl.when(jnp.logical_not(mine))
            def _():
                put(outgoing.at[expo, strip], both)

            @pl.when(mine)
            def _():
                put(strips[expo].at[band_rows(me), :], both)

        def dispatch(expo, index, head, start):
            strip, to, mine = target(index, head)

            @pl.when(jnp.logical_not(mine))
            def _():
                copy = strip_copy(expo, strip, me, to)
                copy.start() if start else copy.wait_send()

    def over_group(group, *actions):
        expo, head, first, end = group

        def step(index, carry):
            for action in actions:
                action(expo, index, head)
            return carry

        lax.fori_loop(first, end, step, 0)

    def begin(expo, index, head):
        dispatch(expo, index, head, True)

    def finish_send(expo, index, head):
        dispatch(expo, index, head, False)

    def send_stat(step, carry):
        stat_copy(me, step).start()
        return carry

    weigh(0, 1)
    loads[0].wait()
    loads[1].wait()
    for expo in range(exposures):
        if expo > 0:
            weigh(expo, 1)
        loads[2 + 2 * expo].wait()
        loads[3 + 2 * expo].wait()
        correct(expo)
        if expo == 0:
            if relay:
                over_group(groups[0], prepare)
            pl.semaphore_wait(barrier, parts + visits - 2)
            if relay:
                over_group(groups[0], begin)
    for group in groups[1 if relay else 0 : 2 if relay else 1]:
        over_group(group, prepare, begin)
    lax.fori_loop(1, parts, send_stat, 0)
    for group in groups[2 if relay else 1 :]:
        over_group(group, prepare, begin)

    for expo in range(exposures):
        weigh(expo, 0)

        def build(block, carry, expo=expo):
            at = pl.multiple_of(block * BLOCK, BLOCK)
            first = window_start(at, frame_len, row_window, ROW_ALIGN)
            rowk[expo, pl.ds(at, BLOCK), :] = banded(taps[expo, 0, :, pl.ds(at, BLOCK)], first, row_window).T
            return carry

        lax.fori_loop(0, frame_len // BLOCK, build, 0)

    def wait_stat(step, carry):
        stat_copy(lax.rem(me + step, parts), step).wait()
        return carry

    lax.fori_loop(1, parts, wait_stat, 0)
    sums = jnp.sum(jnp.sum(stats[...], axis=0), axis=1, keepdims=True)
    weights, full = [], []
    for expo in range(exposures):
        count = sums[exposures + expo : exposures + expo + 1, :]
        weights.append(count / (sums[expo : expo + 1, :] + 1e-05 * count))
        full.append(jnp.where(2.0 * count >= float(frame_len * frame_len), 1.0, 0.0))

    def warp(expo, at, source):
        first = window_start(at, frame_len, row_window, ROW_ALIGN)
        return jnp.dot(
            rowk[expo, pl.ds(at, BLOCK), :],
            source[pl.ds(first, row_window), :],
            preferred_element_type=jnp.float32,
        )

    def block_rows(block):
        return pl.ds(pl.multiple_of(block * BLOCK, BLOCK), BLOCK)

    if relay:
        half_rows = 2 * band
        fill_strip = lax.select(inner, far_strip, me)

        def half_at(index, side):
            return pl.ds(pl.multiple_of(index * n_ty * band + side * half_rows, half_rows), half_rows)

        for expo in range(exposures):
            _, k = column_kernel(expo, fill_strip)
            cover = jnp.sum(k.astype(jnp.float32), axis=0, keepdims=True).astype(jnp.bfloat16)
            cover = cover.astype(jnp.float32) * full[expo]
            cover = jnp.broadcast_to(cover, (half_rows, width)).astype(jnp.bfloat16)
            blank = jnp.zeros((half_rows, width), jnp.bfloat16)

            @pl.when(inner)
            def _(expo=expo, cover=cover, blank=blank):
                for index in range(n_tx):
                    auxs[expo][half_at(index, 1 - high), 0:width] = blank
                    auxs[expo][half_at(index, 1 - high), width : 2 * width] = blank
                    fills[expo][half_at(index, 1 - high), :] = blank
                    fills[expo][half_at(index, high), :] = cover

            @pl.when(outer)
            def _(expo=expo, cover=cover, blank=blank):
                for index in range(n_tx):
                    strips[expo][half_at(index, 1 - high), 0:width] = blank
                    strips[expo][half_at(index, 1 - high), width : 2 * width] = cover

        def half_band(index):
            return lax.div(index, 2) * n_ty + high * 2 + lax.rem(index, 2)

        def aux_sum_copy(block):
            at = pl.multiple_of((1 - vi) * own + block * BLOCK, BLOCK)
            return pltpu.make_async_remote_copy(
                src_ref=aux_totals.at[pl.ds(at, BLOCK), :],
                dst_ref=aux_partial.at[block_rows(block), :],
                send_sem=aux_send.at[block],
                recv_sem=aux_sum_recv.at[block],
                device_id=(1 - vi, ti, yi),
                device_id_type=MESH,
            )

        def relay_copy(block):
            return pltpu.make_async_remote_copy(
                src_ref=relay_out.at[block_rows(block), :],
                dst_ref=relay_in.at[block_rows(block), :],
                send_sem=relay_send.at[block],
                recv_sem=relay_recv.at[block],
                device_id=(vi, ti, far_y),
                device_id_type=MESH,
            )

        def aux_row(at):
            at = pl.multiple_of(at, BLOCK)
            value = cover = 0.0
            for expo in range(exposures):
                both = warp(expo, at, auxs[expo])
                value = value + weights[expo] * both[:, 0:width]
                cover = cover + weights[expo] * (both[:, width : 2 * width] - warp(expo, at, fills[expo]))
            aux_totals[pl.ds(at, BLOCK), 0:width] = value
            aux_totals[pl.ds(at, BLOCK), width : 2 * width] = cover

        @pl.when(inner)
        def _():
            for expo in range(exposures):

                def wait_aux(index, carry, expo=expo):
                    source = half_band(index)

                    @pl.when(source != me)
                    def _():
                        strip_copy(expo, 0, source, (vi, ti, yi), True).wait_recv()

                    return carry

                lax.fori_loop(0, parts // 2, wait_aux, 0)

            def other_half(block, carry):
                aux_row((1 - vi) * own + block * BLOCK)
                aux_sum_copy(block).start()
                return carry

            def own_half(block, carry):
                at = pl.multiple_of(vi * own + block * BLOCK, BLOCK)
                aux_row(at)
                aux_sum_copy(block).wait()
                total = aux_totals[pl.ds(at, BLOCK), :] + aux_partial[block_rows(block), :]
                relay_out[block_rows(block), :] = total.astype(jnp.bfloat16)
                relay_copy(block).start()
                return carry

            lax.fori_loop(0, blocks, other_half, 0)
            lax.fori_loop(0, blocks, own_half, 0)

    def sum_copy(step, block):
        to = lax.rem(vi + step, visits)
        at = pl.multiple_of(to * own + block * BLOCK, BLOCK)
        return pltpu.make_async_remote_copy(
            src_ref=totals.at[pl.ds(at, BLOCK), :],
            dst_ref=partial.at[step, block_rows(block), :],
            send_sem=sum_send.at[step, block],
            recv_sem=sum_recv.at[step, block],
            device_id=(to, ti, yi),
            device_id_type=MESH,
        )

    for expo in range(exposures):

        def wait_strip(step, carry, expo=expo):
            source = lax.rem(me + step, parts)
            if relay:

                @pl.when(inner | (lax.div(lax.rem(source, n_ty), 2) == high))
                def _():
                    strip_copy(expo, 0, source, (vi, ti, yi)).wait_recv()

            else:
                strip_copy(expo, 0, source, (vi, ti, yi)).wait_recv()
            return carry

        lax.fori_loop(1, parts, wait_strip, 0)
        last = expo == exposures - 1

        def row(at, expo=expo):
            at = pl.multiple_of(at, BLOCK)
            warped = weights[expo] * warp(expo, at, strips[expo])
            rows = pl.ds(at, BLOCK)
            totals[rows, :] = warped if expo == 0 else totals[rows, :] + warped

        def row_step(index, carry, row=row, last=last):
            step, block = lax.div(index, blocks) + 1, lax.rem(index, blocks)
            row(lax.rem(vi + step, visits) * own + block * BLOCK)
            if last:
                sum_copy(step, block).start()
            return carry

        def own_row(block, carry, row=row):
            row(vi * own + block * BLOCK)
            return carry

        lax.fori_loop(0, (visits - 1) * blocks, row_step, 0)
        lax.fori_loop(0, blocks, own_row, 0)

    def finish(block, carry):
        total = totals[pl.ds(pl.multiple_of(vi * own + block * BLOCK, BLOCK), BLOCK), :]
        for step in range(1, visits):
            sum_copy(step, block).wait()
            total = total + partial[step, block_rows(block), :]
        out[block_rows(block), :] = total[:, 0:width] / jnp.maximum(total[:, width : 2 * width], 1.0)
        return carry

    if relay:

        @pl.when(outer)
        def _():
            def receive(block, carry):
                relay_copy(block).wait_recv()
                at = pl.ds(pl.multiple_of(vi * own + block * BLOCK, BLOCK), BLOCK)
                totals[at, :] = totals[at, :] + relay_in[block_rows(block), :].astype(jnp.float32)
                return carry

            lax.fori_loop(0, blocks, receive, 0)

    lax.fori_loop(0, blocks, finish, 0)

    for group in groups:
        over_group(group, finish_send)
    if relay:

        @pl.when(inner)
        def _():
            def sent(block, carry):
                relay_copy(block).wait_send()
                return carry

            lax.fori_loop(0, blocks, sent, 0)


def shards(n_visit, n_tx, n_ty, raw, dark, flat, mask, offsets, scales, fracs):
    exposures, band, frame_len = raw.shape
    parts = n_tx * n_ty
    width = frame_len // parts
    own = frame_len // n_visit
    blocks = own // BLOCK
    relay = n_visit == 2 and n_ty == 4 and exposures == 2
    row_window = window_size(frame_len, ROW_ALIGN)
    smem = pl.BlockSpec(memory_space=pltpu.SMEM)
    vmem = pl.BlockSpec(memory_space=pltpu.VMEM)
    dims = (exposures, parts, band, frame_len, n_visit, n_tx, n_ty, relay)
    dma = pltpu.SemaphoreType.DMA
    scratch = [
        pltpu.VMEM(raw.shape, raw.dtype),
        pltpu.VMEM(dark.shape, dark.dtype),
        pltpu.VMEM(flat.shape, flat.dtype),
        pltpu.VMEM(mask.shape, mask.dtype),
        pltpu.VMEM((exposures, 2, 8, frame_len), jnp.float32),
        pltpu.VMEM((exposures, frame_len, row_window), jnp.bfloat16),
        pltpu.VMEM((exposures, 2 * band, frame_len), jnp.bfloat16),
        pltpu.VMEM((exposures, parts, band, 2 * width), jnp.bfloat16),
        pltpu.VMEM((parts, 2 * exposures, 128), jnp.float32),
        pltpu.VMEM((frame_len, 2 * width), jnp.float32),
        pltpu.VMEM((n_visit, own, 2 * width), jnp.float32),
    ]
    scratch += [pltpu.VMEM((frame_len, 2 * width), jnp.bfloat16)] * exposures
    scratch += [
        dma((2 + 2 * exposures,)),
        dma((exposures, parts)),
        dma((exposures, parts)),
        dma((parts,)),
        dma((parts,)),
        dma((n_visit, blocks)),
        dma((n_visit, blocks)),
    ]
    if relay:
        scratch += [pltpu.VMEM((frame_len, 2 * width), jnp.bfloat16)] * exposures
        scratch += [pltpu.VMEM((frame_len, width), jnp.bfloat16)] * exposures
        scratch += [
            pltpu.VMEM((frame_len, 2 * width), jnp.float32),
            pltpu.VMEM((own, 2 * width), jnp.float32),
            pltpu.VMEM((own, 2 * width), jnp.bfloat16),
            pltpu.VMEM((own, 2 * width), jnp.bfloat16),
            dma((exposures, parts)),
            dma((blocks,)),
            dma((blocks,)),
            dma((blocks,)),
            dma((blocks,)),
        ]
    return pl.pallas_call(
        functools.partial(kernel, dims),
        out_shape=jax.ShapeDtypeStruct((own, width), jnp.float32),
        in_specs=[smem] * 3 + [pl.BlockSpec(memory_space=pl.ANY)] * 4,
        out_specs=vmem,
        scratch_shapes=scratch,
        compiler_params=pltpu.CompilerParams(
            collective_id=0, has_side_effects=True, vmem_limit_bytes=60000000
        ),
    )(offsets, scales, fracs, raw, dark, flat, mask)


def solution(mesh):
    in_specs = (
        P("visit", ("tx", "ty"), None),
        P(("tx", "ty"), None),
        P(("tx", "ty"), None),
        P("visit", ("tx", "ty"), None),
        P("visit", None),
        P("visit", None),
        P("visit", None),
    )
    out_specs = P("visit", ("tx", "ty"))
    body = functools.partial(shards, mesh.shape["visit"], mesh.shape["tx"], mesh.shape["ty"])
    return jax.shard_map(body, mesh=mesh, in_specs=in_specs, out_specs=out_specs, check_vma=False)
```
